256 devices in a mesh: dom: 32 (over x, z), cls: 4 (over y), own: 2 (over core).
Axes of the slice: x: 4, y: 4, z: 8, core: 2. Of those that a mesh axis runs over, the one named last changes fastest.
Arguments:
- images: bfloat16 [12288, 4096], P('dom'), may hold values from -6 to 6
- templates: bfloat16 [4, 1152, 4096], P('cls', ('dom', 'own')), may hold values from -0.09375 to 0.09375
- offsets: int32 [12288, 4], P('dom'), may hold values from 0 to 63
- groups: int32 [12288], P('dom'), may hold values from 0 to 15
- prior_block: int32 [12288], P('dom'), may hold values from 0 to 17
- group_weight: float32 [16], replicated, may hold values from 0.5 to 64
- class_log_prior: float32 [4], replicated, may hold values from -1 to 1
Outputs:
- class_post: float32 [12288, 4], P('dom', 'cls')
- class_sums: float32 [4, 1152, 4096], P('cls', ('dom', 'own'))
The draws below stay inside these ranges and needn't reach their ends.
All inputs are finite; a program needn't handle non-finite values.
Results may differ from the reference program's by a relative error of at most 0.0065.
Values may be sent and summed in bfloat16 or wider, within the bound.
No kernel may reach another device: no remote copies, remote signals or barrier semaphores. Data moves between devices by JAX's collectives and lax.ppermute only.
A program may use at most 128 MiB of HBM per device.

```python
import math
import jax
import jax.numpy as jnp
from jax import lax

SIDE = 64
PIX = 4096
SHIFTS = 4
CLASSES = 4
ORIENT = 1152
ORIENT_PER_BLOCK = 64
GROUPS = 16
NPART = 12288


def place_ends(drawn, stream_key, least, top_value):
    extent = drawn.shape
    spot = [jax.random.randint(jax.random.fold_in(stream_key, axis), (), 0, extent[axis]) for axis in range(len(extent))]
    drawn = drawn.at[tuple(spot)].set(least)
    longest = extent.index(max(extent))
    spot[longest] = (spot[longest] + 1) % extent[longest]
    return drawn.at[tuple(spot)].set(top_value)


def level_of(rng, shape, pieces, least, top_value):
    gain = 1.0
    for dim, blocks in pieces:
        heights = jax.random.uniform(jax.random.fold_in(jax.random.fold_in(rng, 6), dim), (blocks,), jnp.float32, least / len(pieces), top_value / len(pieces))
        gain = gain * jnp.repeat(jnp.exp(heights), shape[dim] // blocks).reshape((-1,) + (1,) * (len(shape) - 1 - dim))
    return gain


def centred(rng, dims, width, limit, pieces=(), held_as=jnp.bfloat16):
    factor_of = level_of(rng, dims, pieces, -0.22, 0.18) if pieces else 1.0
    values = jax.random.normal(rng, dims, jnp.float32) * width * factor_of
    return jnp.minimum(jnp.maximum(values, -limit), limit).astype(held_as)


def setup_inputs(seed: int = 0) -> dict:
    keys = jax.random.split(jax.random.key(seed), 8)
    return {
        "images": centred(keys[0], (NPART, PIX), 1.0, 6.0, ((0, 32),)),
        "templates": centred(keys[1], (CLASSES, ORIENT, PIX), PIX ** -0.5, 0.09375, ((0, 4), (1, 64))),
        "offsets": place_ends(jax.random.randint(keys[2], (NPART, SHIFTS), 0, SIDE), jax.random.fold_in(keys[2], 1), 0, SIDE - 1).astype(jnp.int32),
        "groups": place_ends(jax.random.randint(keys[3], (NPART,), 0, GROUPS), jax.random.fold_in(keys[3], 1), 0, GROUPS - 1).astype(jnp.int32),
        "prior_block": place_ends(jax.random.randint(keys[4], (NPART,), 0, ORIENT // ORIENT_PER_BLOCK), jax.random.fold_in(keys[4], 1), 0, (ORIENT // ORIENT_PER_BLOCK) - 1).astype(jnp.int32),
        "group_weight": jnp.clip(jnp.exp(jax.random.uniform(keys[5], (GROUPS,), jnp.float32, math.log(0.5), math.log(64.0))), 0.5, 64.0),
        "class_log_prior": jnp.clip(jax.random.uniform(keys[6], (CLASSES,), jnp.float32, -1.0, 1.0), -1.0, 1.0),
    }


BLOCK_PRIOR_GAIN = 1.5


def reference(images, templates, offsets, groups, prior_block, group_weight, class_log_prior):
    rows_block = min(256, NPART)
    signal_energy = jnp.sum(jnp.square(templates.astype(jnp.float32)), axis=-1)
    orient_block_index = jnp.arange(ORIENT, dtype=jnp.int32) // ORIENT_PER_BLOCK
    table = templates.reshape(CLASSES * ORIENT, PIX)
    pixel_index = jnp.arange(PIX, dtype=jnp.int32)
    count_blocks = NPART // rows_block

    def add_block(running, inputs):
        image_block, offset_block, group_block, log_prior_rows = inputs
        index_grid = (pixel_index[None, None, :] + SIDE * offset_block[:, :, None]) % PIX
        row_ids = jnp.arange(rows_block, dtype=jnp.int32)[:, None, None]
        shifted = image_block[row_ids, index_grid]
        flattened = shifted.reshape(rows_block * SHIFTS, PIX)
        cross_correlation = jnp.dot(flattened, table.T, preferred_element_type=jnp.float32)
        cross_correlation = cross_correlation.reshape(rows_block, SHIFTS, CLASSES, ORIENT)
        noise_variance = group_weight[group_block]
        prior_gain = BLOCK_PRIOR_GAIN * (orient_block_index[None, :] == log_prior_rows[:, None]).astype(jnp.float32)
        match_score = noise_variance[:, None, None, None] * (cross_correlation - 0.5 * signal_energy[None, None]) + class_log_prior[None, None, :, None] + prior_gain[:, None, None, :]
        peak_value = jnp.max(match_score, axis=(1, 2, 3), keepdims=True)
        exps = jnp.exp(match_score - peak_value)
        mass_total = jnp.sum(exps, axis=(1, 2, 3), keepdims=True)
        posterior = exps / mass_total
        class_part = jnp.sum(posterior, axis=(1, 3))
        weight16 = posterior.astype(jnp.bfloat16).reshape(rows_block * SHIFTS, CLASSES * ORIENT)
        added = jnp.dot(weight16.T, flattened, preferred_element_type=jnp.float32)
        return running + added.reshape(CLASSES, ORIENT, PIX), class_part

    inputs = (images.reshape(count_blocks, rows_block, PIX),
              offsets.reshape(count_blocks, rows_block, SHIFTS),
              groups.reshape(count_blocks, rows_block),
              prior_block.reshape(count_blocks, rows_block))
    start_sums = jnp.zeros((CLASSES, ORIENT, PIX), jnp.float32)
    class_sums, class_parts = lax.scan(add_block, start_sums, inputs)
    class_post = class_parts.reshape(NPART, CLASSES)
    return class_post, class_sums
```

```python
import functools

import jax
import jax.numpy as jnp
from jax import lax
from jax.experimental import pallas as pl
from jax.experimental.pallas import tpu as pltpu
from jax.sharding import Mesh, PartitionSpec as P

SIDE = 64
ORIENT_PER_BLOCK = 64
BLOCK_PRIOR_GAIN = 1.5
XS = 4
ZS = 8
LEAD = 8
LAST = 4
VMEM = 56 * 1024 * 1024


def shift_kernel(off_ref, img_ref, out_ref):
    image = img_ref[...]
    turned = jnp.concatenate([image[:, SIDE:], image[:, :SIDE]], axis=1)
    offsets = off_ref[...]

    def pick(amount, bit, yes, no):
        flag = ((amount >> bit) & 1).astype(jnp.float32).astype(jnp.bfloat16)
        return jnp.where(jnp.broadcast_to(flag, image.shape) > 0, yes, no)

    for s in range(out_ref.shape[0]):
        amount = offsets[:, s : s + 1]
        cur = pick(amount, 0, turned, image)
        for bit in range(1, 6):
            lanes = SIDE << bit
            rolled = jnp.concatenate([cur[:, lanes:], cur[:, :lanes]], axis=1)
            cur = pick(amount, bit, rolled, cur)
        out_ref[s] = cur


def make_shifted(images, offsets):
    count, pixels = images.shape
    shifts = offsets.shape[1]
    tile = 32
    return pl.pallas_call(
        shift_kernel,
        out_shape=jax.ShapeDtypeStruct((shifts, count, pixels), jnp.bfloat16),
        grid=(count // tile,),
        in_specs=[
            pl.BlockSpec((tile, shifts), lambda i: (i, 0)),
            pl.BlockSpec((tile, pixels), lambda i: (i, 0)),
        ],
        out_specs=pl.BlockSpec((shifts, tile, pixels), lambda i: (0, i, 0)),
        compiler_params=pltpu.CompilerParams(vmem_limit_bytes=VMEM),
        cost_estimate=pl.CostEstimate(
            flops=20 * count * pixels * shifts, bytes_accessed=2 * count * pixels * (1 + shifts), transcendentals=0
        ),
        name="shift",
    )(offsets, images)


def score_kernel(*refs, starts):
    count = len(starts)
    bias_ref, noise_ref, prior_ref, block_ref, img_ref = refs[:5]
    piece_refs = refs[5 : 5 + count]
    exps_ref, stat_ref, table_ref, energy_ref = refs[5 + count :]
    shifts, tile, pixels = img_ref.shape

    @pl.when(pl.program_id(0) == 0)
    def _():
        for start, piece in zip(starts, piece_refs):
            table_ref[start : start + piece.shape[0], :] = piece[...]
        total = jnp.zeros((table_ref.shape[0], 128), jnp.float32)
        for c in range(0, pixels, 128):
            part = table_ref[:, c : c + 128].astype(jnp.float32)
            total = total + part * part
        energy_ref[...] = 0.5 * jnp.sum(total, axis=1, keepdims=True)

    noise = noise_ref[...]
    gain = jnp.where(block_ref[...] == prior_ref[...], BLOCK_PRIOR_GAIN, 0.0) + bias_ref[0]
    half_energy = energy_ref[...]
    table = table_ref[...]
    peak = None
    for s in range(0, shifts, 2):
        pair = img_ref[s : s + 2].reshape(2 * tile, pixels)
        corr = lax.dot_general(table, pair, (((1,), (1,)), ((), ())), preferred_element_type=jnp.float32)
        for j in range(2):
            score = noise * (corr[:, j * tile : (j + 1) * tile] - half_energy) + gain
            exps_ref[s + j] = score
            top = jnp.max(score, axis=0, keepdims=True)
            peak = top if peak is None else jnp.maximum(peak, top)
    total = jnp.zeros_like(peak)
    for s in range(shifts):
        exps = jnp.exp(exps_ref[s] - peak)
        exps_ref[s] = exps
        total = total + jnp.sum(exps, axis=0, keepdims=True)
    stat_ref[0:1, :] = peak
    stat_ref[1:2, :] = total


def scores(bias, noise, prior, block, table_pieces, shifted):
    shifts, count, pixels = shifted.shape
    starts, orient = [], 0
    for piece in table_pieces:
        starts.append(orient)
        orient += piece.shape[0]
    tile = 128
    return pl.pallas_call(
        functools.partial(score_kernel, starts=tuple(starts)),
        out_shape=(
            jax.ShapeDtypeStruct((shifts, orient, count), jnp.float32),
            jax.ShapeDtypeStruct((2, count), jnp.float32),
        ),
        grid=(count // tile,),
        in_specs=[
            pl.BlockSpec(memory_space=pltpu.SMEM),
            pl.BlockSpec((1, tile), lambda i: (0, i)),
            pl.BlockSpec((1, tile), lambda i: (0, i)),
            pl.BlockSpec((orient, 1), lambda i: (0, 0)),
            pl.BlockSpec((shifts, tile, pixels), lambda i: (0, i, 0)),
        ]
        + [pl.BlockSpec(piece.shape, lambda i: (0, 0)) for piece in table_pieces],
        out_specs=(
            pl.BlockSpec((shifts, orient, tile), lambda i: (0, 0, i)),
            pl.BlockSpec((2, tile), lambda i: (0, i)),
        ),
        scratch_shapes=[pltpu.VMEM((orient, pixels), jnp.bfloat16), pltpu.VMEM((orient, 1), jnp.float32)],
        compiler_params=pltpu.CompilerParams(vmem_limit_bytes=VMEM),
        cost_estimate=pl.CostEstimate(
            flops=2 * shifts * count * pixels * orient,
            bytes_accessed=2 * shifts * count * pixels + 2 * orient * pixels + 4 * shifts * count * orient,
            transcendentals=shifts * count * orient,
        ),
        name="scores",
    )(bias, noise, prior, block, shifted, *table_pieces)


def project_kernel(*refs, others, keep):
    stat_refs = refs[: others + 1]
    exps_ref, img_ref = refs[others + 1 : others + 3]
    out_refs = refs[others + 3 : -2]
    post_ref, weight_ref = refs[-2:]
    shifts, count, width = img_ref.shape

    @pl.when(pl.program_id(0) == 0)
    def _():
        peak = stat_refs[0][0:1, :]
        for ref in stat_refs[1:]:
            peak = jnp.maximum(peak, ref[0:1, :])
        parts = [ref[1:2, :] * jnp.exp(ref[0:1, :] - peak) for ref in stat_refs]
        mass = parts[0]
        for part in parts[1:]:
            mass = mass + part
        post_ref[...] = (parts[0] + parts[1]) / mass
        factor = jnp.exp(stat_refs[0][0:1, :] - peak) / mass
        for s in range(shifts):
            exps = jnp.concatenate([exps_ref[s, start:stop, :] for start, stop in keep], axis=0)
            weight_ref[:, s * count : (s + 1) * count] = (exps * factor).astype(jnp.bfloat16)

    image = img_ref[...].reshape(shifts * count, width)
    sums = jnp.dot(weight_ref[...], image, preferred_element_type=jnp.float32)
    row = 0
    for ref in out_refs:
        ref[...] = sums[row : row + ref.shape[0]].astype(ref.dtype)
        row += ref.shape[0]


def project(stats, exps, shifted, keep, outs):
    shifts, count, pixels = shifted.shape
    orient = exps.shape[1]
    width = 512
    return pl.pallas_call(
        functools.partial(project_kernel, others=len(stats) - 1, keep=tuple(keep)),
        out_shape=tuple(jax.ShapeDtypeStruct((size, pixels), kind) for size, kind in outs)
        + (jax.ShapeDtypeStruct((1, count), jnp.float32),),
        grid=(pixels // width,),
        in_specs=[pl.BlockSpec(stat.shape, lambda i: (0, 0)) for stat in stats]
        + [
            pl.BlockSpec(exps.shape, lambda i: (0, 0, 0)),
            pl.BlockSpec((shifts, count, width), lambda i: (0, 0, i)),
        ],
        out_specs=tuple(pl.BlockSpec((size, width), lambda i: (0, i)) for size, _ in outs)
        + (pl.BlockSpec((1, count), lambda i: (0, 0)),),
        scratch_shapes=[pltpu.VMEM((orient, shifts * count), jnp.bfloat16)],
        compiler_params=pltpu.CompilerParams(vmem_limit_bytes=VMEM),
        cost_estimate=pl.CostEstimate(
            flops=2 * shifts * count * pixels * orient,
            bytes_accessed=2 * shifts * count * pixels + 4 * orient * pixels + 4 * shifts * count * orient,
            transcendentals=0,
        ),
        name="project",
    )(*stats, exps, shifted)


def hop(axis, size, by):
    return axis, [(i, (i + by) % size) for i in range(size)]


def exchange(messages, together=()):
    held = lax.optimization_barrier(tuple(value for value, _ in messages) + tuple(together))
    sent = tuple(lax.ppermute(value, route[0], route[1]) for value, (_, route) in zip(held, messages))
    return lax.optimization_barrier(sent)


def orient_index(per_device):
    x, own = lax.axis_index("x"), lax.axis_index("c")
    dx = jnp.arange(XS, dtype=jnp.int32)
    z = jnp.arange(ZS, dtype=jnp.int32)
    owner = z[:, None] + ((x - dx) % XS)[None, :] * ZS
    row = owner[:, :, None] * (2 * per_device) + own * per_device + jnp.arange(per_device, dtype=jnp.int32)
    lead = row[:, :, :LEAD].transpose(1, 0, 2)
    return jnp.concatenate([lead.reshape(-1), row[:, :, LEAD:].reshape(-1)])


def share_stats(stats):
    messages = []
    for dy, dc in [(0, 1), (1, 0), (3, 0), (1, 1), (3, 1), (2, 0), (2, 1)]:
        pairs = [(y * 2 + c, (y + dy) % 4 * 2 + (c + dc) % 2) for y in range(4) for c in range(2)]
        messages.append((stats, (("y", "c"), pairs)))
    return (stats,) + exchange(messages)


def row_plan(per_device):
    follow = per_device - LEAD
    start = XS * ZS * LEAD

    def lead(z, dx):
        first = (dx * ZS + z) * LEAD
        return (first, first + LEAD)

    def rest(z, dx, low, high):
        first = start + (z * XS + dx) * follow - LEAD
        return (first + low, first + high)

    def block(dx, zs):
        plan = []
        for z in zs:
            plan += [lead(z, dx), rest(z, dx, LEAD, per_device - LAST)]
        return plan

    low, high = range(ZS // 2), range(ZS // 2, ZS)
    direct = [rest(z, dx, per_device - LAST, per_device) for z in range(ZS) for dx in range(XS)]
    plan = direct + block(2, low) + block(1, high) + block(2, high) + block(3, low)
    return plan + block(1, low) + block(3, high) + block(0, low) + block(0, high)


def gather_templates(rows, images, offsets):
    lead, follow = rows[:LEAD], rows[LEAD:]
    near = exchange([(follow, hop("x", XS, d)) for d in range(1, XS)])
    near = jnp.concatenate((follow,) + near, axis=0)
    near, lead = lax.optimization_barrier((near, lead))
    table = lax.all_gather(near, "z", axis=0, tiled=True)
    p_0 = lax.all_gather(lead, "z", axis=0, tiled=True)
    shifted = make_shifted(images, offsets)
    p_1, p_3 = exchange([(p_0, hop("x", XS, 1)), (p_0, hop("x", XS, -1))])
    cut = p_0.shape[0] // 2
    p_2 = exchange([(p_1[:cut], hop("x", XS, 1)), (p_3[cut:], hop("x", XS, -1))], (shifted,))
    return [p_0, p_1, p_2[0], p_2[1], p_3, table], shifted


def shards(images, templates, offsets, groups, prior_block, group_weight, class_log_prior):
    per_device, pixels = templates.shape[1:]
    table, shifted = gather_templates(templates[0], images, offsets)
    onehot = groups[:, None] == jnp.arange(group_weight.shape[0], dtype=jnp.int32)[None, :]
    noise = jnp.sum(jnp.where(onehot, group_weight[None, :], 0.0), axis=1)[None, :]
    bias = lax.dynamic_slice_in_dim(class_log_prior, lax.axis_index("y"), 1, 0)
    block = (orient_index(per_device) // ORIENT_PER_BLOCK)[:, None]
    exps, stats = scores(bias, noise, prior_block[None, :], block, table, shifted)
    stats = share_stats(stats)
    half, wide = jnp.bfloat16, jnp.float32
    turn = ZS * (per_device - LAST)
    cut = turn // 2
    outs = [(XS * ZS * LAST, wide), (turn, half), (turn, half), (turn, wide), (turn, wide)]
    direct, to_left, to_right, onward, own, post = project(stats, exps, shifted, row_plan(per_device), outs)
    direct = lax.psum_scatter(direct, "z", scatter_dimension=0, tiled=True)
    from_right, from_left = exchange([(to_left, hop("x", XS, -1)), (to_right, hop("x", XS, 1))])
    low = (onward[:cut] + from_right[:cut].astype(wide)).astype(half)
    high = (onward[cut:] + from_left[:cut].astype(wide)).astype(half)
    low, high = exchange([(low, hop("x", XS, -1)), (high, hop("x", XS, 1))])
    first = (own[:cut] + from_left[cut:].astype(wide) + low.astype(wide)).astype(half)
    second = (own[cut:] + from_right[cut:].astype(wide) + high.astype(wide)).astype(half)
    sums = jnp.concatenate([first, second], axis=0).reshape(ZS, -1, pixels // 4)
    sums = lax.all_to_all(sums, "z", 0, 0, tiled=True)
    sums = jnp.sum(sums.astype(wide), axis=0).reshape(-1, pixels)
    direct = direct.reshape(XS, LAST, pixels)
    arrived = exchange([(direct[d], hop("x", XS, -d)) for d in range(1, XS)])
    last = direct[0] + arrived[0] + arrived[1] + arrived[2]
    out = jnp.concatenate([sums, last], axis=0)
    return (post.reshape(-1, 1), out[None])


def solution(mesh):
    grid = Mesh(mesh.devices.reshape(XS, ZS, 4, 2), ("x", "z", "y", "c"))
    dom = ("x", "z")
    placed = (
        P(dom, None),
        P("y", ("x", "z", "c"), None),
        P(dom, None),
        P(dom),
        P(dom),
        P(),
        P(),
    )
    return jax.shard_map(
        shards,
        mesh=grid,
        in_specs=placed,
        out_specs=(P(dom, "y"), P("y", ("x", "z", "c"), None)),
        check_vma=False,
    )
```

```python
import functools

import jax
import jax.numpy as jnp
from jax import lax
from jax.experimental import pallas as pl
from jax.experimental.pallas import tpu as pltpu
from jax.sharding import Mesh, PartitionSpec as P

SIDE = 64
ORIENT_PER_BLOCK = 64
BLOCK_PRIOR_GAIN = 1.5
XS = 4
ZS = 8
LEAD = 8
LAST = 6
VMEM = 56 * 1024 * 1024


def shift_kernel(off_ref, img_ref, out_ref):
    image = img_ref[...]
    turned = jnp.concatenate([image[:, SIDE:], image[:, :SIDE]], axis=1)
    offsets = off_ref[...]

    def pick(amount, bit, yes, no):
        flag = ((amount >> bit) & 1).astype(jnp.float32).astype(jnp.bfloat16)
        return jnp.where(jnp.broadcast_to(flag, image.shape) > 0, yes, no)

    for s in range(out_ref.shape[0]):
        amount = offsets[:, s : s + 1]
        cur = pick(amount, 0, turned, image)
        for bit in range(1, 6):
            lanes = SIDE << bit
            rolled = jnp.concatenate([cur[:, lanes:], cur[:, :lanes]], axis=1)
            cur = pick(amount, bit, rolled, cur)
        out_ref[s] = cur


def make_shifted(images, offsets):
    count, pixels = images.shape
    shifts = offsets.shape[1]
    tile = 32
    return pl.pallas_call(
        shift_kernel,
        out_shape=jax.ShapeDtypeStruct((shifts, count, pixels), jnp.bfloat16),
        grid=(count // tile,),
        in_specs=[
            pl.BlockSpec((tile, shifts), lambda i: (i, 0)),
            pl.BlockSpec((tile, pixels), lambda i: (i, 0)),
        ],
        out_specs=pl.BlockSpec((shifts, tile, pixels), lambda i: (0, i, 0)),
        compiler_params=pltpu.CompilerParams(vmem_limit_bytes=VMEM),
        cost_estimate=pl.CostEstimate(
            flops=20 * count * pixels * shifts, bytes_accessed=2 * count * pixels * (1 + shifts), transcendentals=0
        ),
        name="shift",
    )(offsets, images)


def score_kernel(*refs, starts):
    count = len(starts)
    bias_ref, noise_ref, prior_ref, block_ref, img_ref = refs[:5]
    piece_refs = refs[5 : 5 + count]
    exps_ref, stat_ref, table_ref, energy_ref = refs[5 + count :]
    shifts, tile, pixels = img_ref.shape

    @pl.when(pl.program_id(0) == 0)
    def _():
        for start, piece in zip(starts, piece_refs):
            table_ref[start : start + piece.shape[0], :] = piece[...]
        total = jnp.zeros((table_ref.shape[0], 128), jnp.float32)
        for c in range(0, pixels, 128):
            part = table_ref[:, c : c + 128].astype(jnp.float32)
            total = total + part * part
        energy_ref[...] = 0.5 * jnp.sum(total, axis=1, keepdims=True)

    noise = noise_ref[...]
    gain = jnp.where(block_ref[...] == prior_ref[...], BLOCK_PRIOR_GAIN, 0.0) + bias_ref[0]
    half_energy = energy_ref[...]
    table = table_ref[...]
    peak = None
    for s in range(0, shifts, 2):
        pair = img_ref[s : s + 2].reshape(2 * tile, pixels)
        corr = lax.dot_general(table, pair, (((1,), (1,)), ((), ())), preferred_element_type=jnp.float32)
        for j in range(2):
            score = noise * (corr[:, j * tile : (j + 1) * tile] - half_energy) + gain
            exps_ref[s + j] = score
            top = jnp.max(score, axis=0, keepdims=True)
            peak = top if peak is None else jnp.maximum(peak, top)
    total = jnp.zeros_like(peak)
    for s in range(shifts):
        exps = jnp.exp(exps_ref[s] - peak)
        exps_ref[s] = exps
        total = total + jnp.sum(exps, axis=0, keepdims=True)
    stat_ref[0:1, :] = peak
    stat_ref[1:2, :] = total


def scores(bias, noise, prior, block, table_pieces, shifted):
    shifts, count, pixels = shifted.shape
    starts, orient = [], 0
    for piece in table_pieces:
        starts.append(orient)
        orient += piece.shape[0]
    tile = 128
    return pl.pallas_call(
        functools.partial(score_kernel, starts=tuple(starts)),
        out_shape=(
            jax.ShapeDtypeStruct((shifts, orient, count), jnp.float32),
            jax.ShapeDtypeStruct((2, count), jnp.float32),
        ),
        grid=(count // tile,),
        in_specs=[
            pl.BlockSpec(memory_space=pltpu.SMEM),
            pl.BlockSpec((1, tile), lambda i: (0, i)),
            pl.BlockSpec((1, tile), lambda i: (0, i)),
            pl.BlockSpec((orient, 1), lambda i: (0, 0)),
            pl.BlockSpec((shifts, tile, pixels), lambda i: (0, i, 0)),
        ]
        + [pl.BlockSpec(piece.shape, lambda i: (0, 0)) for piece in table_pieces],
        out_specs=(
            pl.BlockSpec((shifts, orient, tile), lambda i: (0, 0, i)),
            pl.BlockSpec((2, tile), lambda i: (0, i)),
        ),
        scratch_shapes=[pltpu.VMEM((orient, pixels), jnp.bfloat16), pltpu.VMEM((orient, 1), jnp.float32)],
        compiler_params=pltpu.CompilerParams(vmem_limit_bytes=VMEM),
        cost_estimate=pl.CostEstimate(
            flops=2 * shifts * count * pixels * orient,
            bytes_accessed=2 * shifts * count * pixels + 2 * orient * pixels + 4 * shifts * count * orient,
            transcendentals=shifts * count * orient,
        ),
        name="scores",
    )(bias, noise, prior, block, shifted, *table_pieces)


def project_kernel(*refs, keep):
    cls_ref, all_ref, own_ref, exps_ref, img_ref = refs[:5]
    out_refs = refs[5:-2]
    post_ref, weight_ref = refs[-2:]
    shifts, count, width = img_ref.shape

    @pl.when(pl.program_id(0) == 0)
    def _():
        peaks = all_ref[:, 0, :]
        peak = jnp.max(peaks, axis=0, keepdims=True)
        parts = all_ref[:, 1, :] * jnp.exp(peaks - peak)
        mass = jnp.sum(parts, axis=0, keepdims=True)
        member = lax.broadcasted_iota(jnp.int32, parts.shape, 0) // 2 == cls_ref[0]
        post_ref[...] = jnp.sum(jnp.where(member, parts, 0.0), axis=0, keepdims=True) / mass
        factor = jnp.exp(own_ref[0:1, :] - peak) / mass
        for s in range(shifts):
            exps = jnp.concatenate([exps_ref[s, start:stop, :] for start, stop in keep], axis=0)
            weight_ref[:, s * count : (s + 1) * count] = (exps * factor).astype(jnp.bfloat16)

    image = img_ref[...].reshape(shifts * count, width)
    sums = jnp.dot(weight_ref[...], image, preferred_element_type=jnp.float32)
    row = 0
    for ref in out_refs:
        ref[...] = sums[row : row + ref.shape[0]].astype(ref.dtype)
        row += ref.shape[0]


def project(cls_index, gathered, own, exps, shifted, keep, outs):
    shifts, count, pixels = shifted.shape
    orient = exps.shape[1]
    width = 512
    return pl.pallas_call(
        functools.partial(project_kernel, keep=tuple(keep)),
        out_shape=tuple(jax.ShapeDtypeStruct((size, pixels), kind) for size, kind in outs)
        + (jax.ShapeDtypeStruct((1, count), jnp.float32),),
        grid=(pixels // width,),
        in_specs=[
            pl.BlockSpec(memory_space=pltpu.SMEM),
            pl.BlockSpec(gathered.shape, lambda i: (0, 0, 0)),
            pl.BlockSpec(own.shape, lambda i: (0, 0)),
            pl.BlockSpec(exps.shape, lambda i: (0, 0, 0)),
            pl.BlockSpec((shifts, count, width), lambda i: (0, 0, i)),
        ],
        out_specs=tuple(pl.BlockSpec((size, width), lambda i: (0, i)) for size, _ in outs)
        + (pl.BlockSpec((1, count), lambda i: (0, 0)),),
        scratch_shapes=[pltpu.VMEM((orient, shifts * count), jnp.bfloat16)],
        compiler_params=pltpu.CompilerParams(vmem_limit_bytes=VMEM),
        cost_estimate=pl.CostEstimate(
            flops=2 * shifts * count * pixels * orient,
            bytes_accessed=2 * shifts * count * pixels + 4 * orient * pixels + 4 * shifts * count * orient,
            transcendentals=0,
        ),
        name="project",
    )(cls_index, gathered, own, exps, shifted)


def hop(axis, size, by):
    return axis, [(i, (i + by) % size) for i in range(size)]


def exchange(messages, together=()):
    held = lax.optimization_barrier(tuple(value for value, _ in messages) + tuple(together))
    sent = tuple(lax.ppermute(value, route[0], route[1]) for value, (_, route) in zip(held, messages))
    return lax.optimization_barrier(sent)


def orient_index(per_device):
    x, own = lax.axis_index("x"), lax.axis_index("c")
    dx = jnp.arange(XS, dtype=jnp.int32)
    z = jnp.arange(ZS, dtype=jnp.int32)
    owner = z[:, None] + ((x - dx) % XS)[None, :] * ZS
    row = owner[:, :, None] * (2 * per_device) + own * per_device + jnp.arange(per_device, dtype=jnp.int32)
    lead = row[:, :, :LEAD].transpose(1, 0, 2)
    return jnp.concatenate([lead.reshape(-1), row[:, :, LEAD:].reshape(-1)])


def row_plan(per_device):
    follow = per_device - LEAD
    start = XS * ZS * LEAD

    def lead(z, dx):
        first = (dx * ZS + z) * LEAD
        return (first, first + LEAD)

    def rest(z, dx, low, high):
        first = start + (z * XS + dx) * follow - LEAD
        return (first + low, first + high)

    def block(dx, zs):
        plan = []
        for z in zs:
            plan.append(lead(z, dx))
            if LEAD < per_device - LAST:
                plan.append(rest(z, dx, LEAD, per_device - LAST))
        return plan

    low, high = range(ZS // 2), range(ZS // 2, ZS)
    direct = [rest(z, dx, per_device - LAST, per_device) for z in range(ZS) for dx in range(XS)]
    plan = direct + block(2, low) + block(1, high) + block(2, high) + block(3, low)
    return plan + block(1, low) + block(3, high) + block(0, low) + block(0, high)


def gather_templates(rows, images, offsets):
    lead, follow = rows[:LEAD], rows[LEAD:]
    near = exchange([(follow, hop("x", XS, d)) for d in range(1, XS)])
    p_0 = lax.all_to_all(jnp.tile(lead, (ZS, 1)), "z", 0, 0, tiled=True)
    near = jnp.concatenate((follow,) + near, axis=0)
    near, p_0 = lax.optimization_barrier((near, p_0))
    table = lax.all_gather(near, "z", axis=0, tiled=True)
    shifted = make_shifted(images, offsets)
    p_1, p_3 = exchange([(p_0, hop("x", XS, 1)), (p_0, hop("x", XS, -1))])
    cut = p_0.shape[0] // 2
    p_2 = exchange([(p_1[:cut], hop("x", XS, 1)), (p_3[cut:], hop("x", XS, -1))], (shifted,))
    return [p_0, p_1, p_2[0], p_2[1], p_3, table], shifted


def shards(images, templates, offsets, groups, prior_block, group_weight, class_log_prior):
    per_device, pixels = templates.shape[1:]
    table, shifted = gather_templates(templates[0], images, offsets)
    onehot = groups[:, None] == jnp.arange(group_weight.shape[0], dtype=jnp.int32)[None, :]
    noise = jnp.sum(jnp.where(onehot, group_weight[None, :], 0.0), axis=1)[None, :]
    cls_index = lax.axis_index("y")
    bias = lax.dynamic_slice_in_dim(class_log_prior, cls_index, 1, 0)
    block = (orient_index(per_device) // ORIENT_PER_BLOCK)[:, None]
    exps, stats = scores(bias, noise, prior_block[None, :], block, table, shifted)
    gathered = lax.all_to_all(jnp.broadcast_to(stats[None], (8,) + stats.shape), ("y", "c"), 0, 0, tiled=True)
    half, wide = jnp.bfloat16, jnp.float32
    turn = ZS * (per_device - LAST)
    cut = turn // 2
    outs = [(XS * ZS * LAST, wide), (turn, half), (turn, half), (turn, wide), (turn, wide)]
    direct, to_left, to_right, onward, own, post = project(
        cls_index[None], gathered, stats, exps, shifted, row_plan(per_device), outs
    )
    direct = lax.psum_scatter(direct, "z", scatter_dimension=0, tiled=True)
    from_right, from_left = exchange([(to_left, hop("x", XS, -1)), (to_right, hop("x", XS, 1))])
    low = (onward[:cut] + from_right[:cut].astype(wide)).astype(half)
    high = (onward[cut:] + from_left[:cut].astype(wide)).astype(half)
    low, high = exchange([(low, hop("x", XS, -1)), (high, hop("x", XS, 1))])
    first = (own[:cut] + from_left[cut:].astype(wide) + low.astype(wide)).astype(half)
    second = (own[cut:] + from_right[cut:].astype(wide) + high.astype(wide)).astype(half)
    sums = jnp.concatenate([first, second], axis=0).reshape(ZS, -1, pixels // 4)
    sums = lax.all_to_all(sums, "z", 0, 0, tiled=True)
    sums = jnp.sum(sums.astype(wide), axis=0).reshape(-1, pixels)
    direct = direct.reshape(XS, LAST, pixels)
    arrived = exchange([(direct[d], hop("x", XS, -d)) for d in range(1, XS)])
    last = direct[0] + arrived[0] + arrived[1] + arrived[2]
    out = jnp.concatenate([sums, last], axis=0)
    return (post.reshape(-1, 1), out[None])


def solution(mesh):
    grid = Mesh(mesh.devices.reshape(XS, ZS, 4, 2), ("x", "z", "y", "c"))
    dom = ("x", "z")
    placed = (
        P(dom, None),
        P("y", ("x", "z", "c"), None),
        P(dom, None),
        P(dom),
        P(dom),
        P(),
        P(),
    )
    return jax.shard_map(
        shards,
        mesh=grid,
        in_specs=placed,
        out_specs=(P(dom, "y"), P("y", ("x", "z", "c"), None)),
        check_vma=False,
    )
```

```python
import functools

import jax
import jax.numpy as jnp
from jax import lax
from jax.experimental import pallas as pl
from jax.experimental.pallas import tpu as pltpu
from jax.sharding import Mesh, PartitionSpec as P

SIDE = 64
ORIENT_PER_BLOCK = 64
BLOCK_PRIOR_GAIN = 1.5
XS = 4
ZS = 8
LEAD = 8
LAST = 6
VMEM = 56 * 1024 * 1024


def shift_kernel(off_ref, img_ref, out_ref):
    image = img_ref[...]
    turned = jnp.concatenate([image[:, SIDE:], image[:, :SIDE]], axis=1)
    offsets = off_ref[...]

    def pick(amount, bit, yes, no):
        flag = ((amount >> bit) & 1).astype(jnp.float32).astype(jnp.bfloat16)
        return jnp.where(jnp.broadcast_to(flag, image.shape) > 0, yes, no)

    for s in range(out_ref.shape[0]):
        amount = offsets[:, s : s + 1]
        cur = pick(amount, 0, turned, image)
        for bit in range(1, 6):
            lanes = SIDE << bit
            rolled = jnp.concatenate([cur[:, lanes:], cur[:, :lanes]], axis=1)
            cur = pick(amount, bit, rolled, cur)
        out_ref[s] = cur


def make_shifted(images, offsets):
    count, pixels = images.shape
    shifts = offsets.shape[1]
    tile = 32
    return pl.pallas_call(
        shift_kernel,
        out_shape=jax.ShapeDtypeStruct((shifts, count, pixels), jnp.bfloat16),
        grid=(count // tile,),
        in_specs=[
            pl.BlockSpec((tile, shifts), lambda i: (i, 0)),
            pl.BlockSpec((tile, pixels), lambda i: (i, 0)),
        ],
        out_specs=pl.BlockSpec((shifts, tile, pixels), lambda i: (0, i, 0)),
        compiler_params=pltpu.CompilerParams(vmem_limit_bytes=VMEM),
        cost_estimate=pl.CostEstimate(
            flops=20 * count * pixels * shifts, bytes_accessed=2 * count * pixels * (1 + shifts), transcendentals=0
        ),
        name="shift",
    )(offsets, images)


def score_kernel(*refs, starts, follows):
    count = len(starts)
    before_ref = refs[5 + count] if follows else None
    bias_ref, noise_ref, prior_ref, block_ref, img_ref = refs[:5]
    piece_refs = refs[5 : 5 + count]
    exps_ref, stat_ref, table_ref, energy_ref = refs[-4:]
    shifts, tile, pixels = img_ref.shape

    @pl.when(pl.program_id(0) == 0)
    def _():
        for start, piece in zip(starts, piece_refs):
            table_ref[start : start + piece.shape[0], :] = piece[...]
        total = jnp.zeros((table_ref.shape[0], 128), jnp.float32)
        for c in range(0, pixels, 128):
            part = table_ref[:, c : c + 128].astype(jnp.float32)
            total = total + part * part
        energy_ref[...] = 0.5 * jnp.sum(total, axis=1, keepdims=True)

    noise = noise_ref[...]
    gain = jnp.where(block_ref[...] == prior_ref[...], BLOCK_PRIOR_GAIN, 0.0) + bias_ref[0]
    half_energy = energy_ref[...]
    table = table_ref[...]
    peak = None
    for s in range(0, shifts, 2):
        pair = img_ref[s : s + 2].reshape(2 * tile, pixels)
        corr = lax.dot_general(table, pair, (((1,), (1,)), ((), ())), preferred_element_type=jnp.float32)
        for j in range(2):
            score = noise * (corr[:, j * tile : (j + 1) * tile] - half_energy) + gain
            exps_ref[s + j] = score
            top = jnp.max(score, axis=0, keepdims=True)
            peak = top if peak is None else jnp.maximum(peak, top)
    total = jnp.zeros_like(peak)
    if follows:
        peak = jnp.maximum(peak, before_ref[0:1, :])
        total = before_ref[1:2, :] * jnp.exp(before_ref[0:1, :] - peak)
    for s in range(shifts):
        exps = jnp.exp(exps_ref[s] - peak)
        exps_ref[s] = exps
        total = total + jnp.sum(exps, axis=0, keepdims=True)
    stat_ref[0:1, :] = peak
    stat_ref[1:2, :] = total


def scores(bias, noise, prior, block, table_pieces, shifted, name, before=()):
    shifts, count, pixels = shifted.shape
    starts, orient = [], 0
    for piece in table_pieces:
        starts.append(orient)
        orient += piece.shape[0]
    tile = 128
    return pl.pallas_call(
        functools.partial(score_kernel, starts=tuple(starts), follows=len(before) > 0),
        out_shape=(
            jax.ShapeDtypeStruct((shifts, orient, count), jnp.float32),
            jax.ShapeDtypeStruct((2, count), jnp.float32),
        ),
        grid=(count // tile,),
        in_specs=[
            pl.BlockSpec(memory_space=pltpu.SMEM),
            pl.BlockSpec((1, tile), lambda i: (0, i)),
            pl.BlockSpec((1, tile), lambda i: (0, i)),
            pl.BlockSpec((orient, 1), lambda i: (0, 0)),
            pl.BlockSpec((shifts, tile, pixels), lambda i: (0, i, 0)),
        ]
        + [pl.BlockSpec(piece.shape, lambda i: (0, 0)) for piece in table_pieces]
        + [pl.BlockSpec((2, tile), lambda i: (0, i)) for _ in before],
        out_specs=(
            pl.BlockSpec((shifts, orient, tile), lambda i: (0, 0, i)),
            pl.BlockSpec((2, tile), lambda i: (0, i)),
        ),
        scratch_shapes=[pltpu.VMEM((orient, pixels), jnp.bfloat16), pltpu.VMEM((orient, 1), jnp.float32)],
        compiler_params=pltpu.CompilerParams(vmem_limit_bytes=VMEM),
        cost_estimate=pl.CostEstimate(
            flops=2 * shifts * count * pixels * orient,
            bytes_accessed=2 * shifts * count * pixels + 2 * orient * pixels + 4 * shifts * count * orient,
            transcendentals=shifts * count * orient,
        ),
        name=name,
    )(bias, noise, prior, block, shifted, *table_pieces, *before)


def project_kernel(*refs, keep):
    cls_ref, all_ref, lead_ref, own_ref, lead_exps_ref, exps_ref, img_ref = refs[:7]
    out_refs = refs[7:-2]
    rows_lead = lead_exps_ref.shape[1]
    post_ref, weight_ref = refs[-2:]
    shifts, count, width = img_ref.shape

    @pl.when(pl.program_id(0) == 0)
    def _():
        peaks = all_ref[:, 0, :]
        peak = jnp.max(peaks, axis=0, keepdims=True)
        parts = all_ref[:, 1, :] * jnp.exp(peaks - peak)
        mass = jnp.sum(parts, axis=0, keepdims=True)
        member = lax.broadcasted_iota(jnp.int32, parts.shape, 0) // 2 == cls_ref[0]
        post_ref[...] = jnp.sum(jnp.where(member, parts, 0.0), axis=0, keepdims=True) / mass
        lead_factor = jnp.exp(lead_ref[0:1, :] - peak) / mass
        factor = jnp.exp(own_ref[0:1, :] - peak) / mass
        for s in range(shifts):
            lead = lead_exps_ref[s] * lead_factor
            rest = exps_ref[s] * factor
            picked = []
            for start, stop in keep:
                if stop <= rows_lead:
                    picked.append(lead[start:stop])
                else:
                    picked.append(rest[start - rows_lead : stop - rows_lead])
            weight = jnp.concatenate(picked, axis=0)
            weight_ref[:, s * count : (s + 1) * count] = weight.astype(jnp.bfloat16)

    image = img_ref[...].reshape(shifts * count, width)
    sums = jnp.dot(weight_ref[...], image, preferred_element_type=jnp.float32)
    row = 0
    for ref in out_refs:
        ref[...] = sums[row : row + ref.shape[0]].astype(ref.dtype)
        row += ref.shape[0]


def project(cls_index, gathered, lead, own, lead_exps, exps, shifted, keep, outs):
    shifts, count, pixels = shifted.shape
    orient = lead_exps.shape[1] + exps.shape[1]
    width = 1024
    return pl.pallas_call(
        functools.partial(project_kernel, keep=tuple(keep)),
        out_shape=tuple(jax.ShapeDtypeStruct((size, pixels), kind) for size, kind in outs)
        + (jax.ShapeDtypeStruct((1, count), jnp.float32),),
        grid=(pixels // width,),
        in_specs=[
            pl.BlockSpec(memory_space=pltpu.SMEM),
            pl.BlockSpec(gathered.shape, lambda i: (0, 0, 0)),
            pl.BlockSpec(lead.shape, lambda i: (0, 0)),
            pl.BlockSpec(own.shape, lambda i: (0, 0)),
            pl.BlockSpec(lead_exps.shape, lambda i: (0, 0, 0)),
            pl.BlockSpec(exps.shape, lambda i: (0, 0, 0)),
            pl.BlockSpec((shifts, count, width), lambda i: (0, 0, i)),
        ],
        out_specs=tuple(pl.BlockSpec((size, width), lambda i: (0, i)) for size, _ in outs)
        + (pl.BlockSpec((1, count), lambda i: (0, 0)),),
        scratch_shapes=[pltpu.VMEM((orient, shifts * count), jnp.bfloat16)],
        compiler_params=pltpu.CompilerParams(vmem_limit_bytes=VMEM),
        cost_estimate=pl.CostEstimate(
            flops=2 * shifts * count * pixels * orient,
            bytes_accessed=2 * shifts * count * pixels + 4 * orient * pixels + 4 * shifts * count * orient,
            transcendentals=0,
        ),
        name="project",
    )(cls_index, gathered, lead, own, lead_exps, exps, shifted)


def hop(axis, size, by):
    return axis, [(i, (i + by) % size) for i in range(size)]


def exchange(messages, together=()):
    held = lax.optimization_barrier(tuple(value for value, _ in messages) + tuple(together))
    sent = tuple(lax.ppermute(value, route[0], route[1]) for value, (_, route) in zip(held, messages))
    return lax.optimization_barrier(sent)


def orient_index(per_device):
    x, own = lax.axis_index("x"), lax.axis_index("c")
    dx = jnp.arange(XS, dtype=jnp.int32)
    z = jnp.arange(ZS, dtype=jnp.int32)
    owner = z[:, None] + ((x - dx) % XS)[None, :] * ZS
    row = owner[:, :, None] * (2 * per_device) + own * per_device + jnp.arange(per_device, dtype=jnp.int32)
    lead = row[:, :, :LEAD].transpose(1, 0, 2)
    return jnp.concatenate([lead.reshape(-1), row[:, :, LEAD:].reshape(-1)])


def row_plan(per_device):
    follow = per_device - LEAD
    start = XS * ZS * LEAD

    def lead(z, dx):
        first = (dx * ZS + z) * LEAD
        return (first, first + LEAD)

    def rest(z, dx, low, high):
        first = start + (z * XS + dx) * follow - LEAD
        return (first + low, first + high)

    def block(dx, zs):
        plan = []
        for z in zs:
            plan.append(lead(z, dx))
            if LEAD < per_device - LAST:
                plan.append(rest(z, dx, LEAD, per_device - LAST))
        return plan

    low, high = range(ZS // 2), range(ZS // 2, ZS)
    direct = [rest(z, dx, per_device - LAST, per_device) for z in range(ZS) for dx in range(XS)]
    plan = direct + block(2, low) + block(1, high) + block(2, high) + block(3, low)
    return plan + block(1, low) + block(3, high) + block(0, low) + block(0, high)


def gather_templates(rows, images, offsets):
    lead, follow = rows[:LEAD], rows[LEAD:]
    near = exchange([(follow, hop("x", XS, d)) for d in range(1, XS)])
    p_0 = lax.all_to_all(jnp.tile(lead, (ZS, 1)), "z", 0, 0, tiled=True)
    near = jnp.concatenate((follow,) + near, axis=0)
    near, p_0 = lax.optimization_barrier((near, p_0))
    table = lax.all_gather(near, "z", axis=0, tiled=True)
    shifted = make_shifted(images, offsets)
    p_1, p_3 = exchange([(p_0, hop("x", XS, 1)), (p_0, hop("x", XS, -1))])
    cut = p_0.shape[0] // 2
    p_2 = exchange([(p_1[:cut], hop("x", XS, 1)), (p_3[cut:], hop("x", XS, -1))], (shifted,))
    return [p_0, p_1, p_2[0], p_2[1], p_3, table], shifted


def shards(images, templates, offsets, groups, prior_block, group_weight, class_log_prior):
    per_device, pixels = templates.shape[1:]
    table, shifted = gather_templates(templates[0], images, offsets)
    onehot = groups[:, None] == jnp.arange(group_weight.shape[0], dtype=jnp.int32)[None, :]
    noise = jnp.sum(jnp.where(onehot, group_weight[None, :], 0.0), axis=1)[None, :]
    cls_index = lax.axis_index("y")
    bias = lax.dynamic_slice_in_dim(class_log_prior, cls_index, 1, 0)
    block = (orient_index(per_device) // ORIENT_PER_BLOCK)[:, None]
    rows_lead = XS * ZS * LEAD
    prior = prior_block[None, :]
    lead_exps, lead = scores(bias, noise, prior, block[:rows_lead], table[:-1], shifted, "scores_lead")
    exps, stats = scores(bias, noise, prior, block[rows_lead:], table[-1:], shifted, "scores_rest", (lead,))
    gathered = lax.all_to_all(jnp.broadcast_to(stats[None], (8,) + stats.shape), ("y", "c"), 0, 0, tiled=True)
    half, wide = jnp.bfloat16, jnp.float32
    turn = ZS * (per_device - LAST)
    cut = turn // 2
    outs = [(XS * ZS * LAST, wide), (turn, half), (turn, half), (turn, wide), (turn, wide)]
    direct, to_left, to_right, onward, own, post = project(
        cls_index[None], gathered, lead, stats, lead_exps, exps, shifted, row_plan(per_device), outs
    )
    direct = lax.psum_scatter(direct, "z", scatter_dimension=0, tiled=True)
    from_right, from_left = exchange([(to_left, hop("x", XS, -1)), (to_right, hop("x", XS, 1))])
    low = (onward[:cut] + from_right[:cut].astype(wide)).astype(half)
    high = (onward[cut:] + from_left[:cut].astype(wide)).astype(half)
    low, high = exchange([(low, hop("x", XS, -1)), (high, hop("x", XS, 1))])
    first = (own[:cut] + from_left[cut:].astype(wide) + low.astype(wide)).astype(half)
    second = (own[cut:] + from_right[cut:].astype(wide) + high.astype(wide)).astype(half)
    sums = jnp.concatenate([first, second], axis=0).reshape(ZS, -1, pixels // 4)
    sums = lax.all_to_all(sums, "z", 0, 0, tiled=True)
    sums = jnp.sum(sums.astype(wide), axis=0).reshape(-1, pixels)
    direct = direct.reshape(XS, LAST, pixels)
    arrived = exchange([(direct[d], hop("x", XS, -d)) for d in range(1, XS)])
    last = direct[0] + arrived[0] + arrived[1] + arrived[2]
    out = jnp.concatenate([sums, last], axis=0)
    return (post.reshape(-1, 1), out[None])


def solution(mesh):
    grid = Mesh(mesh.devices.reshape(XS, ZS, 4, 2), ("x", "z", "y", "c"))
    dom = ("x", "z")
    placed = (
        P(dom, None),
        P("y", ("x", "z", "c"), None),
        P(dom, None),
        P(dom),
        P(dom),
        P(),
        P(),
    )
    return jax.shard_map(
        shards,
        mesh=grid,
        in_specs=placed,
        out_specs=(P(dom, "y"), P("y", ("x", "z", "c"), None)),
        check_vma=False,
    )
```
